32 devices in a mesh: gx: 8 (over z, core), gy: 4 (over y, x).
Axes of the slice: x: 2, y: 2, z: 4, core: 2. Of those that a mesh axis runs over, the one named last changes fastest.
Arguments:
- rhs_field: float32 [128, 64, 128], P('gx', 'gy'), may hold values from -10 to 10
- diag_blocks: bfloat16 [128, 64, 128, 128], P('gx', 'gy'), may hold values from -1 to 4, as said below
- face_lift: bfloat16 [4, 128, 128], replicated, may hold values from -0.5 to 0.5
- face_state: int32 [128, 64, 4], P('gx', 'gy'), may hold values from 0 to 2
- restrict_basis: float32 [128, 8], replicated, may hold values from -0.5 to 0.5
- coarse_inverse: float32 [128, 64, 8, 8], P('gx', 'gy'), may hold values from -0.4 to 1.2
Outputs:
- solution_field: float32 [128, 64, 128], P('gx', 'gy')
- hessenberg: float32 [3, 2], replicated
The draws below stay inside these ranges and needn't reach their ends.
Inputs may be any that keep to these rules, and one draw needn't show every extreme that they name: `diag_blocks`: each block has diagonal entries between 2 and 4 and small off-diagonal entries.
All inputs are finite; a program needn't handle non-finite values.
Results may differ from the reference program's by a relative error of at most 0.0023.
Values may be sent and summed in bfloat16 or wider, within the bound.
A program may use at most 64 MiB of HBM per device.

```python
import math
import jax
import jax.numpy as jnp
from jax import lax

NODES = 128
COARSE = 8
NX = 128
NY = 64


def draw_rhs_field(key, part):
    first_key = jax.random.fold_in(key, 0)
    slope_term = 0.5 + jnp.arange(NY, dtype=jnp.float32) / NY
    base = jnp.clip(jax.random.normal(first_key, (NX, NY, NODES), jnp.float32), -6.0, 6.0)
    return base + slope_term[None, :, None]


def draw_diag_blocks(key, part):
    first_key, second_key = jax.random.split(key)
    diag_vals = jnp.exp(jax.random.uniform(first_key, (NX, NY, NODES), jnp.float32, math.log(2.0), math.log(4.0)))
    offdiag = jnp.clip(jax.random.normal(second_key, (NX, NY, NODES, NODES), jnp.float32), -4.0, 4.0)
    offdiag = offdiag / math.sqrt(NODES)
    identity = jnp.eye(NODES, dtype=jnp.float32)
    return (offdiag * (1.0 - identity) + identity * diag_vals[..., None]).astype(jnp.bfloat16)


def draw_coarse_inverse(key, part):
    first_key, second_key = jax.random.split(key)
    diag_vals = jnp.exp(jax.random.uniform(first_key, (NX, NY, COARSE), jnp.float32, math.log(0.4), math.log(1.2)))
    offdiag = jnp.clip(0.1 * jax.random.normal(second_key, (NX, NY, COARSE, COARSE), jnp.float32), -0.4, 0.4)
    identity = jnp.eye(COARSE, dtype=jnp.float32)
    return offdiag * (1.0 - identity) + identity * diag_vals[..., None]


def set_ends(values, stream_key, smallest, top_value):
    dims = values.shape
    spot = [jax.random.randint(jax.random.fold_in(stream_key, axis), (), 0, dims[axis]) for axis in range(len(dims))]
    values = values.at[tuple(spot)].set(smallest)
    longest = dims.index(max(dims))
    spot[longest] = (spot[longest] + 1) % dims[longest]
    return values.at[tuple(spot)].set(top_value)


def noise(rng, extent, scale, bound, held_as=jnp.bfloat16):
    entries = jax.random.normal(rng, extent, jnp.float32) * scale
    return jnp.minimum(jnp.maximum(entries, -bound), bound).astype(held_as)


def setup_inputs(seed: int = 0) -> dict:
    seeds = jax.random.split(jax.random.key(seed), 7)
    rhs_field = draw_rhs_field(jax.random.fold_in(seeds[6], 71), 0)
    diag_blocks = draw_diag_blocks(jax.random.fold_in(seeds[6], 71), 0)
    face_lift = noise(seeds[2], (4, NODES, NODES), NODES ** -0.5, 0.5)
    face_state = set_ends(jax.random.randint(seeds[3], (NX, NY, 4), 0, 3), jax.random.fold_in(seeds[3], 1), 0, 2).astype(jnp.int32)
    restrict_basis = noise(seeds[4], (NODES, COARSE), NODES ** -0.5, 0.5, jnp.float32)
    coarse_inverse = draw_coarse_inverse(jax.random.fold_in(seeds[6], 71), 0)
    return dict(rhs_field=rhs_field, diag_blocks=diag_blocks, face_lift=face_lift, face_state=face_state, restrict_basis=restrict_basis, coarse_inverse=coarse_inverse)


def apply_operator(field, diag_blocks, face_lift, face_state):
    rounded = field.astype(jnp.bfloat16)

    def row_product(pair):
        return jnp.einsum('ja,jab->jb', pair[0].astype(jnp.float32), pair[1].astype(jnp.float32))
    local_part = lax.map(row_product, (rounded, diag_blocks))
    padded = jnp.pad(rounded, ((1, 1), (1, 1), (0, 0)))
    neighbours = [padded[:-2, 1:-1], padded[2:, 1:-1], padded[1:-1, :-2], padded[1:-1, 2:]]
    zero_block = jnp.zeros_like(rounded)
    selected = []
    for face in range(4):
        state = face_state[:, :, face][:, :, None]
        other = neighbours[face]
        selected.append(jnp.where(state == 1, other, jnp.where(state == 2, other[:, :, ::-1], zero_block)))
    stacked = jnp.concatenate(selected, axis=-1)
    lifted = jnp.dot(stacked.reshape(-1, 4 * NODES), face_lift.reshape(4 * NODES, NODES), preferred_element_type=jnp.float32)
    return local_part + lifted.reshape(field.shape)

def coarse_correct(field, restrict_basis, coarse_inverse):
    high = lax.Precision.HIGHEST
    coarse = jnp.einsum('ija,ak->ijk', field, restrict_basis, precision=high)
    column_mean = lax.optimization_barrier(jnp.mean(coarse, axis=1, keepdims=True))
    centred = coarse - column_mean
    padded = jnp.pad(centred, ((0, 0), (1, 1), (0, 0)))
    smoothed = centred + 0.25 * (padded[:, :-2] + padded[:, 2:])
    solved = jnp.einsum('ijk,ijkl->ijl', smoothed, coarse_inverse, precision=high)
    return field + jnp.einsum('ijl,al->ija', solved, restrict_basis, precision=high)

def least_squares(start_len, hess):
    first = jnp.sqrt(hess[0, 0] ** 2 + hess[1, 0] ** 2)
    cos_one = hess[0, 0] / first
    sin_one = hess[1, 0] / first
    upper = cos_one * hess[0, 1] + sin_one * hess[1, 1]
    lower = -sin_one * hess[0, 1] + cos_one * hess[1, 1]
    second = jnp.sqrt(lower ** 2 + hess[2, 1] ** 2)
    cos_two = lower / second
    coef_two = cos_two * (-sin_one * start_len) / second
    coef_one = (cos_one * start_len - upper * coef_two) / first
    return (coef_one, coef_two)

def reference(rhs_field, diag_blocks, face_lift, face_state, restrict_basis, coarse_inverse):
    start_len = jnp.sqrt(jnp.sum(rhs_field * rhs_field))
    basis = [rhs_field / start_len]
    precon = []
    hess = jnp.zeros((3, 2), jnp.float32)
    for step in range(2):
        precond = coarse_correct(basis[step], restrict_basis, coarse_inverse)
        precon.append(precond)
        image = apply_operator(precond, diag_blocks, face_lift, face_state)
        coeffs = [jnp.sum(vector * image) for vector in basis]
        for index in range(step + 1):
            image = image - coeffs[index] * basis[index]
            hess = hess.at[index, step].set(coeffs[index])
        length = jnp.sqrt(jnp.sum(image * image))
        hess = hess.at[step + 1, step].set(length)
        if step == 0:
            basis.append(image / length)
    coef_one, coef_two = least_squares(start_len, hess)
    return (coef_one * precon[0] + coef_two * precon[1], hess)
```

```python
import functools
import jax
import jax.numpy as jnp
from jax import lax
from jax.experimental import pallas as pl
from jax.experimental.pallas import tpu as pltpu
from jax.sharding import PartitionSpec as P

MESH = pl.DeviceIdType.MESH
F32 = jnp.float32
BF16 = jnp.bfloat16


def hdot(a, b, dims=(((1,), (0,)), ((), ()))):
    return lax.dot_general(a, b, dims, precision=lax.Precision.HIGHEST, preferred_element_type=F32)


def total(x):
    return jnp.sum(jnp.sum(x, axis=0, keepdims=True), axis=1, keepdims=True)


def safe_div(a, b):
    return jnp.where(b > 0, a / jnp.where(b > 0, b, 1.0), 0.0)


def iota(shape, dim):
    return lax.broadcasted_iota(jnp.int32, shape, dim)


def kernel(nx, ny, ti, tj, n, kc, rhs, diag, lift, state, basis, cinv, out, hess_out,
           dvm, wts, masks, cext, wbuf, sends, halos, csend, chalo, msgs,
           dsem, ssem, rsem, msend, mrecv):
    gx = lax.axis_index("gx")
    gy = lax.axis_index("gy")
    me = gx * ny + gy
    count = nx * ny
    elems = ti * tj
    kk = kc * kc

    dcopies = [pltpu.make_async_copy(diag.at[q], dvm.at[q], dsem.at[q]) for q in range(ti)]
    for c in dcopies:
        c.start()

    barrier = pltpu.get_barrier_semaphore()

    def greet(k, carry):
        t = lax.rem(me + k, count)
        pl.semaphore_signal(barrier, inc=1, device_id=(t // ny, lax.rem(t, ny)), device_id_type=MESH)
        return carry

    lax.fori_loop(1, count, greet, 0)

    has_n, has_s, has_w, has_e = gx > 0, gx < nx - 1, gy > 0, gy < ny - 1
    h = 2 * ti + 2 * tj
    o_n, o_s, o_w, o_e = 0, tj, 2 * tj, 2 * tj + 2 * ti
    o_nw = 2 * tj + 4 * ti
    o_ne, o_sw, o_se = o_nw + 8, o_nw + 16, o_nw + 24
    hrows = o_nw + 32
    routes = [
        (has_n, (gx - 1, gy), o_n, o_s, tj),
        (has_s, (gx + 1, gy), o_s, o_n, tj),
        (has_w, (gx, gy - 1), o_w, o_e, 2 * ti),
        (has_e, (gx, gy + 1), o_e, o_w, 2 * ti),
        (jnp.logical_and(has_n, has_w), (gx - 1, gy - 1), o_nw, o_se, 8),
        (jnp.logical_and(has_n, has_e), (gx - 1, gy + 1), o_ne, o_sw, 8),
        (jnp.logical_and(has_s, has_w), (gx + 1, gy - 1), o_sw, o_ne, 8),
        (jnp.logical_and(has_s, has_e), (gx + 1, gy + 1), o_se, o_nw, 8),
    ]
    croutes = [
        (has_n, (gx - 1, gy), 0, tj, tj),
        (has_s, (gx + 1, gy), tj, 0, tj),
        (has_w, (gx, gy - 1), 2 * tj, 2 * tj + ti, ti),
        (has_e, (gx, gy + 1), 2 * tj + ti, 2 * tj, ti),
    ]
    opposite = [1, 0, 3, 2, 7, 6, 5, 4]

    def rim_copies(g):
        return [(ok, pltpu.make_async_remote_copy(
            src_ref=sends.at[g, pl.ds(src, rows)], dst_ref=halos.at[g, pl.ds(dst, rows)],
            send_sem=ssem.at[g, d], recv_sem=rsem.at[g, opposite[d]],
            device_id=dev, device_id_type=MESH)) for d, (ok, dev, src, dst, rows) in enumerate(routes)]

    def coarse_copies():
        return [(ok, pltpu.make_async_remote_copy(
            src_ref=csend.at[pl.ds(src, rows)], dst_ref=chalo.at[pl.ds(dst, rows)],
            send_sem=ssem.at[2, d], recv_sem=rsem.at[2, opposite[d]],
            device_id=dev, device_id_type=MESH)) for d, (ok, dev, src, dst, rows) in enumerate(croutes)]

    def rim_wait(g, which):
        table = routes if g < 2 else croutes
        for d, (ok, dev, src, dst, rows) in enumerate(table):
            @pl.when(ok)
            def _(d=d, dev=dev, src=src, rows=rows):
                if g < 2:
                    s, r = sends.at[g, pl.ds(src, rows)], halos.at[g, pl.ds(src, rows)]
                else:
                    s, r = csend.at[pl.ds(src, rows)], chalo.at[pl.ds(src, rows)]
                c = pltpu.make_async_remote_copy(
                    src_ref=s, dst_ref=r, send_sem=ssem.at[g, d], recv_sem=rsem.at[g, d],
                    device_id=dev, device_id_type=MESH)
                if which == "send":
                    c.wait_send()
                else:
                    c.wait_recv()

    def start_all(copies):
        for ok, c in copies:
            @pl.when(ok)
            def _(c=c):
                c.start()

    def broadcast(g):
        def one(k, carry):
            t = lax.rem(me + k, count)
            pltpu.make_async_remote_copy(
                src_ref=msgs.at[g, me], dst_ref=msgs.at[g, me], send_sem=msend.at[g], recv_sem=mrecv.at[g],
                device_id=(t // ny, lax.rem(t, ny)), device_id_type=MESH).start()
            return carry
        lax.fori_loop(1, count, one, 0)

    def bc_wait(g, which):
        part = msgs.at[g, pl.ds(0, count - 1)]
        c = pltpu.make_async_remote_copy(
            src_ref=part, dst_ref=part, send_sem=msend.at[g], recv_sem=mrecv.at[g],
            device_id=(gx, gy), device_id_type=MESH)
        if which == "send":
            c.wait_send()
        else:
            c.wait_recv()

    def fill_sends(g, ref):
        sends[g, o_n:o_n + tj] = ref[0]
        sends[g, o_s:o_s + tj] = ref[ti - 1]
        sends[g, o_w:o_w + ti] = ref[:, 0, :]
        sends[g, o_w + ti:o_w + 2 * ti] = ref[:, 1, :]
        sends[g, o_e:o_e + ti] = ref[:, tj - 1, :]
        sends[g, o_e + ti:o_e + 2 * ti] = ref[:, tj - 2, :]
        sends[g, o_nw:o_nw + 8] = jnp.broadcast_to(ref[0, 0:1, :], (8, n))
        sends[g, o_ne:o_ne + 8] = jnp.broadcast_to(ref[0, tj - 1:tj, :], (8, n))
        sends[g, o_sw:o_sw + 8] = jnp.broadcast_to(ref[ti - 1, 0:1, :], (8, n))
        sends[g, o_se:o_se + 8] = jnp.broadcast_to(ref[ti - 1, tj - 1:tj, :], (8, n))

    lane1 = iota((1, n), 1)

    def message(values):
        row = jnp.zeros((1, n), F32)
        for p, v in enumerate(values):
            row = jnp.where(lane1 == p, v, row)
        return row

    R = basis[...]
    e1 = (iota((kc, n), 1) // kc == iota((kc, n), 0)).astype(F32)
    e3 = (lax.rem(iota((kc, n), 1), kc) == iota((kc, n), 0)).astype(F32)
    e4 = (lax.rem(iota((n, kc), 0), kc) == iota((n, kc), 1)).astype(F32)
    RT = hdot(R, e3)
    pick = iota((ti, n), 1) // kc == iota((ti, n), 0)

    def packed_rowsum(f3):
        rows = hdot(jnp.sum(f3, axis=1), RT)
        return jnp.sum(jnp.where(pick, rows, 0.0), axis=0, keepdims=True)

    rhs3 = rhs[...]
    rhs2 = rhs3.reshape(elems, n)
    fill_sends(0, rhs)
    csend[0:tj] = cinv[0]
    csend[tj:2 * tj] = cinv[ti - 1]
    csend[2 * tj:2 * tj + ti] = cinv[:, 0, :]
    csend[2 * tj + ti:2 * tj + 2 * ti] = cinv[:, tj - 1, :]
    msgs[0, me, 0:1] = message([total(rhs2 * rhs2)])
    msgs[0, me, 1:2] = packed_rowsum(rhs3)

    pl.semaphore_wait(barrier, count - 1)
    broadcast(0)
    start_all(rim_copies(0))
    start_all(coarse_copies())

    RE = hdot(R, e1)
    RF = hdot(e4, R, (((1,), (1,)), ((), ())))
    G = (lax.rem(iota((n, n), 0), kc) == iota((n, n), 1) // kc).astype(F32)
    flip = (iota((n, n), 0) + iota((n, n), 1) == n - 1).astype(BF16)
    for f in range(4):
        wts[2 * f * n:(2 * f + 1) * n] = lift[f]
        wts[(2 * f + 1) * n:(2 * f + 2) * n] = jnp.dot(flip, lift[f], preferred_element_type=F32).astype(BF16)
    st = state[...]
    for f in range(4):
        col = jnp.broadcast_to(st[:, f:f + 1], (elems, n))
        masks[2 * f] = (col == 1).astype(F32)
        masks[2 * f + 1] = (col == 2).astype(F32)

    hrow = iota((hrows, 1), 0)
    n_i, s_i, w_i, e_i = [v.astype(jnp.int32) for v in (has_n, has_s, has_w, has_e)]
    valid = jnp.where(hrow < o_s, n_i, jnp.where(hrow < o_w, s_i, jnp.where(
        hrow < o_e, w_i, jnp.where(hrow < o_nw, e_i, jnp.where(
            hrow < o_ne, n_i * w_i, jnp.where(hrow < o_sw, n_i * e_i, jnp.where(
                hrow < o_se, s_i * w_i, s_i * e_i))))))) > 0

    jrow = lax.rem(iota((elems, 1), 0), tj)
    trow = iota((tj, 1), 0)

    def spread(col):
        return jnp.broadcast_to(col[:, None, :], (ti, tj, n)).reshape(elems, n)

    def left_of(x, edge):
        return jnp.where(jrow == 0, spread(edge), pltpu.roll(x, 1, 0))

    def right_of(x, edge):
        return jnp.where(jrow == tj - 1, spread(edge), pltpu.roll(x, elems - 1, 0))

    def line_sum(g, line):
        acc = msgs[g, line * ny, 1:2]
        for q in range(1, ny):
            acc = acc + msgs[g, line * ny + q, 1:2]
        return acc

    def three_lines(g):
        return (line_sum(g, gx), line_sum(g, jnp.maximum(gx - 1, 0)), line_sum(g, jnp.minimum(gx + 1, nx - 1)))

    def precondition(f_own, f_halo, lines):
        p_c, p_n, p_s = lines
        stack = jnp.concatenate([
            jnp.where(pick, jnp.broadcast_to(p_c, (ti, n)), 0.0),
            jnp.broadcast_to(jnp.where(lane1 // kc == ti - 1, p_n, 0.0), (8, n)),
            jnp.broadcast_to(jnp.where(lane1 // kc == 0, p_s, 0.0), (8, n))], axis=0)
        mean = hdot(stack, G) * (1.0 / (ny * tj))
        m_c, m_n, m_s = mean[0:ti], mean[ti:ti + 1], mean[ti + 8:ti + 9]
        c_own = hdot(f_own, RE) - spread(m_c)
        c_halo = hdot(f_halo, RE)
        m_halo = jnp.concatenate([
            jnp.broadcast_to(m_n, (tj, n)), jnp.broadcast_to(m_s, (tj, n)), m_c, m_c, m_c, m_c,
            jnp.broadcast_to(m_n, (16, n)), jnp.broadcast_to(m_s, (16, n))], axis=0)
        c_halo = jnp.where(valid, c_halo - m_halo, 0.0)
        c_w1, c_w2 = c_halo[o_w:o_w + ti], c_halo[o_w + ti:o_e]
        c_e1, c_e2 = c_halo[o_e:o_e + ti], c_halo[o_e + ti:o_nw]
        c_n, c_s = c_halo[o_n:o_n + tj], c_halo[o_s:o_s + tj]
        c3 = c_own.reshape(ti, tj, n)
        s_own = c_own + 0.25 * (left_of(c_own, c_w1) + right_of(c_own, c_e1))

        def row_smooth(x, lo, hi):
            left = jnp.where(trow == 0, lo, pltpu.roll(x, 1, 0))
            right = jnp.where(trow == tj - 1, hi, pltpu.roll(x, tj - 1, 0))
            return x + 0.25 * (left + right)
        s_n = row_smooth(c_n, c_halo[o_nw:o_nw + 1], c_halo[o_ne:o_ne + 1])
        s_s = row_smooth(c_s, c_halo[o_sw:o_sw + 1], c_halo[o_se:o_se + 1])
        s_w = c_w1 + 0.25 * (c_w2 + c3[:, 0, :])
        s_e = c_e1 + 0.25 * (c3[:, tj - 1, :] + c_e2)
        z_own = f_own + hdot(s_own * cext[0:elems], RF)
        f_rim = jnp.concatenate([f_halo[o_n:o_w], f_halo[o_w:o_w + ti], f_halo[o_e:o_e + ti]], axis=0)
        ok_rim = jnp.concatenate([valid[o_n:o_w], valid[o_w:o_w + ti], valid[o_e:o_e + ti]], axis=0)
        s_rim = jnp.concatenate([s_n, s_s, s_w, s_e], axis=0)
        z_rim = jnp.where(ok_rim, f_rim + hdot(s_rim * cext[elems:elems + h], RF), 0.0)
        return z_own, z_rim

    def operator(z, z_rim):
        nb = [
            jnp.concatenate([z_rim[0:tj], z[0:elems - tj]], axis=0),
            jnp.concatenate([z[tj:], z_rim[tj:2 * tj]], axis=0),
            left_of(z, z_rim[2 * tj:2 * tj + ti]),
            right_of(z, z_rim[2 * tj + ti:2 * tj + 2 * ti]),
        ]
        cols = []
        for f in range(4):
            cols.append((nb[f] * masks[2 * f]).astype(BF16))
            cols.append((nb[f] * masks[2 * f + 1]).astype(BF16))
        lifted = jnp.dot(jnp.concatenate(cols, axis=1), wts[...], preferred_element_type=F32)
        wbuf[...] = lifted.reshape(ti, tj, n)
        erow = iota((tj, n), 0)
        for q in range(0, ti, 2):
            a = z[q * tj:(q + 1) * tj]
            b = z[(q + 1) * tj:(q + 2) * tj]
            lhs = jnp.concatenate([jnp.concatenate(
                [jnp.where(erow == e, a, 0.0), jnp.where(erow == e, b, 0.0)], axis=0).astype(BF16)
                for e in range(tj)], axis=1)
            rhs_w = jnp.concatenate([dvm[q].reshape(tj * n, n), dvm[q + 1].reshape(tj * n, n)], axis=1)
            prod = jnp.dot(lhs, rhs_w, preferred_element_type=F32)
            wbuf[q] += prod[0:tj, 0:n]
            wbuf[q + 1] += prod[tj:2 * tj, n:2 * n]

    bc_wait(0, "recv")
    rim_wait(0, "recv")
    rim_wait(2, "recv")

    cext[0:elems] = cinv[...].reshape(elems, n)
    cext[elems:elems + h] = chalo[...]
    lens = msgs[0, :, 0, :][:, 0:1]
    start_len = jnp.sqrt(jnp.sum(lens, axis=0, keepdims=True))
    inv_len = 1.0 / start_len
    n_one = lens * inv_len * inv_len
    v1 = rhs2 * inv_len
    v1_halo = jnp.where(valid, halos[0] * inv_len, 0.0)
    lines1 = [p * inv_len for p in three_lines(0)]
    z1, z1_rim = precondition(v1, v1_halo, lines1)
    for c in dcopies:
        c.wait()
    operator(z1, z1_rim)
    fill_sends(1, wbuf)
    start_all(rim_copies(1))
    w1 = wbuf[...].reshape(elems, n)
    own_n1 = total(v1 * v1)
    dot_one = total(v1 * w1)
    p_one = safe_div(dot_one, own_n1)
    gap = w1 - p_one * v1
    msgs[1, me, 0:1] = message([dot_one, p_one, total(gap * gap), own_n1])
    msgs[1, me, 1:2] = packed_rowsum(wbuf[...])
    broadcast(1)
    bc_wait(1, "recv")
    rim_wait(1, "recv")

    X = msgs[1, :, 0, :]
    h11 = jnp.sum(X[:, 0:1], axis=0, keepdims=True)
    dev = X[:, 1:2] - h11
    h21 = jnp.sqrt(jnp.sum(X[:, 2:3] + dev * dev * X[:, 3:4], axis=0, keepdims=True))
    inv21 = 1.0 / h21
    v2 = (w1 - h11 * v1) * inv21
    v2_halo = jnp.where(valid, (halos[1] - h11 * v1_halo) * inv21, 0.0)
    lines2 = [(pw - h11 * pv) * inv21 for pw, pv in zip(three_lines(1), lines1)]
    z2, z2_rim = precondition(v2, v2_halo, lines2)
    operator(z2, z2_rim)
    w2 = wbuf[...].reshape(elems, n)
    alpha = safe_div(total(v1 * v2), own_n1)
    q2 = v2 - alpha * v1
    nq = total(q2 * q2)
    d1 = total(w2 * v1)
    d2 = total(w2 * v2)
    p1 = safe_div(d1, own_n1)
    p2 = safe_div(d2 - alpha * d1, nq)
    gap2 = w2 - p1 * v1 - p2 * q2
    msgs[2, me, 0:1] = message([d1, d2, alpha, nq, p1, p2, total(gap2 * gap2), own_n1])
    msgs[2, me, 1:2] = jnp.zeros((1, n), F32)
    broadcast(2)
    bc_wait(2, "recv")
    Y = msgs[2, :, 0, :]
    h12 = jnp.sum(Y[:, 0:1], axis=0, keepdims=True)
    h22 = jnp.sum(Y[:, 1:2], axis=0, keepdims=True)
    t1 = Y[:, 4:5] - h12 - h22 * Y[:, 2:3]
    t2 = Y[:, 5:6] - h22
    h32 = jnp.sqrt(jnp.sum(t1 * t1 * Y[:, 7:8] + t2 * t2 * Y[:, 3:4] + Y[:, 6:7], axis=0, keepdims=True))

    first = jnp.sqrt(h11 * h11 + h21 * h21)
    cos_one = h11 / first
    sin_one = h21 / first
    upper = cos_one * h12 + sin_one * h22
    lower = -sin_one * h12 + cos_one * h22
    second = jnp.sqrt(lower * lower + h32 * h32)
    cos_two = lower / second
    y2 = cos_two * (-sin_one * start_len) / second
    y1 = (cos_one * start_len - upper * y2) / first
    out[...] = (y1 * z1 + y2 * z2).reshape(ti, tj, n)
    hr, hc = iota((3, 2), 0), iota((3, 2), 1)
    hess_out[...] = jnp.where(
        hr == 0, jnp.where(hc == 0, h11, h12),
        jnp.where(hr == 1, jnp.where(hc == 0, h21, h22), jnp.where(hc == 0, 0.0, h32)))

    for g in range(3):
        bc_wait(g, "send")
        rim_wait(g, "send")


def solution(mesh):
    nx, ny = mesh.shape["gx"], mesh.shape["gy"]

    def body(rhs, diag, lift, state, basis, cinv):
        ti, tj, n = rhs.shape
        kc = basis.shape[1]
        cflat = jnp.pad(cinv.reshape(ti, tj, kc * kc), ((0, 0), (0, 0), (0, n - kc * kc)))
        sflat = state.reshape(ti * tj, 4)
        hrows = 2 * tj + 4 * ti + 32
        h = 2 * ti + 2 * tj
        vm = pl.BlockSpec(memory_space=pltpu.VMEM)
        return pl.pallas_call(
            functools.partial(kernel, nx, ny, ti, tj, n, kc),
            out_shape=(jax.ShapeDtypeStruct((ti, tj, n), F32), jax.ShapeDtypeStruct((3, 2), F32)),
            in_specs=[vm, pl.BlockSpec(memory_space=pl.ANY), vm, vm, vm, vm],
            out_specs=(vm, vm),
            scratch_shapes=[
                pltpu.VMEM((ti, tj, n, n), BF16),
                pltpu.VMEM((8 * n, n), BF16),
                pltpu.VMEM((8, ti * tj, n), F32),
                pltpu.VMEM((ti * tj + h, n), F32),
                pltpu.VMEM((ti, tj, n), F32),
                pltpu.VMEM((2, hrows, n), F32),
                pltpu.VMEM((2, hrows, n), F32),
                pltpu.VMEM((h, n), F32),
                pltpu.VMEM((h, n), F32),
                pltpu.VMEM((3, nx * ny, 2, n), F32),
                pltpu.SemaphoreType.DMA((ti,)),
                pltpu.SemaphoreType.DMA((3, 8)),
                pltpu.SemaphoreType.DMA((3, 8)),
                pltpu.SemaphoreType.DMA((3,)),
                pltpu.SemaphoreType.DMA((3,)),
            ],
            compiler_params=pltpu.CompilerParams(collective_id=0, has_side_effects=True,
                                                 vmem_limit_bytes=40 * 1024 * 1024),
        )(rhs, diag, lift, sflat, basis, cflat)

    in_specs = (P("gx", "gy", None), P("gx", "gy", None, None), P(), P("gx", "gy", None), P(),
                P("gx", "gy", None, None))
    return jax.shard_map(body, mesh=mesh, in_specs=in_specs, out_specs=(P("gx", "gy", None), P()), check_vma=False)
```

```python
import functools
import jax
import jax.numpy as jnp
from jax import lax
from jax.experimental import pallas as pl
from jax.experimental.pallas import tpu as pltpu
from jax.sharding import PartitionSpec as P

MESH = pl.DeviceIdType.MESH
F32 = jnp.float32
BF16 = jnp.bfloat16


def hdot(a, b, dims=(((1,), (0,)), ((), ()))):
    return lax.dot_general(a, b, dims, precision=lax.Precision.HIGHEST, preferred_element_type=F32)


def total(x):
    return jnp.sum(jnp.sum(x, axis=0, keepdims=True), axis=1, keepdims=True)


def safe_div(a, b):
    return jnp.where(b > 0, a / jnp.where(b > 0, b, 1.0), 0.0)


def iota(shape, dim):
    return lax.broadcasted_iota(jnp.int32, shape, dim)


def kernel(nx, ny, ti, tj, n, kc, rhs_h, diag, lift_h, state_h, basis_h, cinv_h, out, hess_out,
           rhs, lift, state, basis, cinv,
           dvm, wts, masks, cext, wbuf, sends, halos, csend, chalo, msgs,
           isem, dsem, ssem, rsem, msend, mrecv):
    gx = lax.axis_index("gx")
    gy = lax.axis_index("gy")
    me = gx * ny + gy
    count = nx * ny
    elems = ti * tj
    kk = kc * kc

    loads = [pltpu.make_async_copy(a, b, isem.at[q]) for q, (a, b) in enumerate(
        ((rhs_h, rhs), (basis_h, basis), (cinv_h, cinv), (state_h, state), (lift_h, lift)))]
    for c in loads:
        c.start()
    dcopies = [pltpu.make_async_copy(diag.at[q], dvm.at[q], dsem.at[q]) for q in range(ti)]
    for c in dcopies:
        c.start()

    barrier = pltpu.get_barrier_semaphore()

    def greet(k, carry):
        t = lax.rem(me + k, count)
        pl.semaphore_signal(barrier, inc=1, device_id=(t // ny, lax.rem(t, ny)), device_id_type=MESH)
        return carry

    lax.fori_loop(1, count, greet, 0)

    has_n, has_s, has_w, has_e = gx > 0, gx < nx - 1, gy > 0, gy < ny - 1
    h = 2 * ti + 2 * tj
    o_n, o_s, o_w, o_e = 0, tj, 2 * tj, 2 * tj + 2 * ti
    o_nw = 2 * tj + 4 * ti
    o_ne, o_sw, o_se = o_nw + 8, o_nw + 16, o_nw + 24
    hrows = o_nw + 32
    routes = [
        (has_n, (gx - 1, gy), o_n, o_s, tj),
        (has_s, (gx + 1, gy), o_s, o_n, tj),
        (has_w, (gx, gy - 1), o_w, o_e, 2 * ti),
        (has_e, (gx, gy + 1), o_e, o_w, 2 * ti),
        (jnp.logical_and(has_n, has_w), (gx - 1, gy - 1), o_nw, o_se, 8),
        (jnp.logical_and(has_n, has_e), (gx - 1, gy + 1), o_ne, o_sw, 8),
        (jnp.logical_and(has_s, has_w), (gx + 1, gy - 1), o_sw, o_ne, 8),
        (jnp.logical_and(has_s, has_e), (gx + 1, gy + 1), o_se, o_nw, 8),
    ]
    croutes = [
        (has_n, (gx - 1, gy), 0, tj, tj),
        (has_s, (gx + 1, gy), tj, 0, tj),
        (has_w, (gx, gy - 1), 2 * tj, 2 * tj + ti, ti),
        (has_e, (gx, gy + 1), 2 * tj + ti, 2 * tj, ti),
    ]
    opposite = [1, 0, 3, 2, 7, 6, 5, 4]

    def rim_copies(g):
        return [(ok, pltpu.make_async_remote_copy(
            src_ref=sends.at[g, pl.ds(src, rows)], dst_ref=halos.at[g, pl.ds(dst, rows)],
            send_sem=ssem.at[g, d], recv_sem=rsem.at[g, opposite[d]],
            device_id=dev, device_id_type=MESH)) for d, (ok, dev, src, dst, rows) in enumerate(routes)]

    def coarse_copies():
        return [(ok, pltpu.make_async_remote_copy(
            src_ref=csend.at[pl.ds(src, rows)], dst_ref=chalo.at[pl.ds(dst, rows)],
            send_sem=ssem.at[2, d], recv_sem=rsem.at[2, opposite[d]],
            device_id=dev, device_id_type=MESH)) for d, (ok, dev, src, dst, rows) in enumerate(croutes)]

    def rim_wait(g, which):
        table = routes if g < 2 else croutes
        for d, (ok, dev, src, dst, rows) in enumerate(table):
            @pl.when(ok)
            def _(d=d, dev=dev, src=src, rows=rows):
                if g < 2:
                    s, r = sends.at[g, pl.ds(src, rows)], halos.at[g, pl.ds(src, rows)]
                else:
                    s, r = csend.at[pl.ds(src, rows)], chalo.at[pl.ds(src, rows)]
                c = pltpu.make_async_remote_copy(
                    src_ref=s, dst_ref=r, send_sem=ssem.at[g, d], recv_sem=rsem.at[g, d],
                    device_id=dev, device_id_type=MESH)
                if which == "send":
                    c.wait_send()
                else:
                    c.wait_recv()

    def start_all(copies):
        for ok, c in copies:
            @pl.when(ok)
            def _(c=c):
                c.start()

    def broadcast(g):
        def one(k, carry):
            t = lax.rem(me + k, count)
            pltpu.make_async_remote_copy(
                src_ref=msgs.at[g, me], dst_ref=msgs.at[g, me], send_sem=msend.at[g], recv_sem=mrecv.at[g],
                device_id=(t // ny, lax.rem(t, ny)), device_id_type=MESH).start()
            return carry
        lax.fori_loop(1, count, one, 0)

    def bc_wait(g, which):
        part = msgs.at[g, pl.ds(0, count - 1)]
        c = pltpu.make_async_remote_copy(
            src_ref=part, dst_ref=part, send_sem=msend.at[g], recv_sem=mrecv.at[g],
            device_id=(gx, gy), device_id_type=MESH)
        if which == "send":
            c.wait_send()
        else:
            c.wait_recv()

    def fill_sends(g, ref):
        sends[g, o_n:o_n + tj] = ref[0]
        sends[g, o_s:o_s + tj] = ref[ti - 1]
        sends[g, o_w:o_w + ti] = ref[:, 0, :]
        sends[g, o_w + ti:o_w + 2 * ti] = ref[:, 1, :]
        sends[g, o_e:o_e + ti] = ref[:, tj - 1, :]
        sends[g, o_e + ti:o_e + 2 * ti] = ref[:, tj - 2, :]
        sends[g, o_nw:o_nw + 8] = jnp.broadcast_to(ref[0, 0:1, :], (8, n))
        sends[g, o_ne:o_ne + 8] = jnp.broadcast_to(ref[0, tj - 1:tj, :], (8, n))
        sends[g, o_sw:o_sw + 8] = jnp.broadcast_to(ref[ti - 1, 0:1, :], (8, n))
        sends[g, o_se:o_se + 8] = jnp.broadcast_to(ref[ti - 1, tj - 1:tj, :], (8, n))

    lane1 = iota((1, n), 1)

    def message(values):
        row = jnp.zeros((1, n), F32)
        for p, v in enumerate(values):
            row = jnp.where(lane1 == p, v, row)
        return row

    e1 = (iota((kc, n), 1) // kc == iota((kc, n), 0)).astype(F32)
    e3 = (lax.rem(iota((kc, n), 1), kc) == iota((kc, n), 0)).astype(F32)
    pick = iota((ti, n), 1) // kc == iota((ti, n), 0)
    loads[0].wait()
    loads[1].wait()
    Rt = basis[...]
    over_first = (((0,), (0,)), ((), ()))
    RT = hdot(Rt, e3, over_first)

    def packed_rowsum(f3):
        rows = hdot(jnp.sum(f3, axis=1), RT)
        return jnp.sum(jnp.where(pick, rows, 0.0), axis=0, keepdims=True)

    rhs3 = rhs[...]
    rhs2 = rhs3.reshape(elems, n)
    fill_sends(0, rhs)
    msgs[0, me, 0:1] = message([total(rhs2 * rhs2)])
    msgs[0, me, 1:2] = packed_rowsum(rhs3)

    pl.semaphore_wait(barrier, count - 1)
    broadcast(0)
    start_all(rim_copies(0))
    loads[2].wait()
    cext[...] = jnp.zeros_like(cext)
    eye = (iota((tj, tj), 0) == iota((tj, tj), 1)).astype(F32)
    for q in range(ti):
        cext[q * tj:(q + 1) * tj, 0:kk] = hdot(eye, cinv[q], (((1,), (1,)), ((), ())))
    c3d = cext[0:elems].reshape(ti, tj, n)
    csend[0:tj] = c3d[0]
    csend[tj:2 * tj] = c3d[ti - 1]
    csend[2 * tj:2 * tj + ti] = c3d[:, 0, :]
    csend[2 * tj + ti:2 * tj + 2 * ti] = c3d[:, tj - 1, :]
    start_all(coarse_copies())

    RE = hdot(Rt, e1, over_first)
    e4 = (lax.rem(iota((n, kc), 0), kc) == iota((n, kc), 1)).astype(F32)
    RF = hdot(e4, Rt)
    G = (lax.rem(iota((n, n), 0), kc) == iota((n, n), 1) // kc).astype(F32)
    flip = (iota((n, n), 0) + iota((n, n), 1) == n - 1).astype(BF16)
    loads[4].wait()
    for f in range(4):
        wts[2 * f * n:(2 * f + 1) * n] = lift[f]
        wts[(2 * f + 1) * n:(2 * f + 2) * n] = jnp.dot(flip, lift[f], preferred_element_type=F32).astype(BF16)
    loads[3].wait()
    own_j = lax.rem(iota((elems, tj), 0), tj) == iota((elems, tj), 1)
    ones = jnp.ones((tj, n), BF16)
    for f in range(4):
        rows = state[:, f, :].astype(F32)
        wide = jnp.broadcast_to(rows[:, None, :], (ti, tj, tj)).reshape(elems, tj)
        col = jnp.dot(jnp.where(own_j, wide, 0.0).astype(BF16), ones, preferred_element_type=F32)
        masks[2 * f] = (col == 1.0).astype(F32)
        masks[2 * f + 1] = (col == 2.0).astype(F32)

    hrow = iota((hrows, 1), 0)
    n_i, s_i, w_i, e_i = [v.astype(jnp.int32) for v in (has_n, has_s, has_w, has_e)]
    valid = jnp.where(hrow < o_s, n_i, jnp.where(hrow < o_w, s_i, jnp.where(
        hrow < o_e, w_i, jnp.where(hrow < o_nw, e_i, jnp.where(
            hrow < o_ne, n_i * w_i, jnp.where(hrow < o_sw, n_i * e_i, jnp.where(
                hrow < o_se, s_i * w_i, s_i * e_i))))))) > 0

    jrow = lax.rem(iota((elems, 1), 0), tj)
    trow = iota((tj, 1), 0)

    def spread(col):
        return jnp.broadcast_to(col[:, None, :], (ti, tj, n)).reshape(elems, n)

    def left_of(x, edge):
        return jnp.where(jrow == 0, spread(edge), pltpu.roll(x, 1, 0))

    def right_of(x, edge):
        return jnp.where(jrow == tj - 1, spread(edge), pltpu.roll(x, elems - 1, 0))

    def line_sum(g, line):
        acc = msgs[g, line * ny, 1:2]
        for q in range(1, ny):
            acc = acc + msgs[g, line * ny + q, 1:2]
        return acc

    def three_lines(g):
        return (line_sum(g, gx), line_sum(g, jnp.maximum(gx - 1, 0)), line_sum(g, jnp.minimum(gx + 1, nx - 1)))

    def precondition(f_own, f_halo, lines):
        p_c, p_n, p_s = lines
        stack = jnp.concatenate([
            jnp.where(pick, jnp.broadcast_to(p_c, (ti, n)), 0.0),
            jnp.broadcast_to(jnp.where(lane1 // kc == ti - 1, p_n, 0.0), (8, n)),
            jnp.broadcast_to(jnp.where(lane1 // kc == 0, p_s, 0.0), (8, n))], axis=0)
        mean = hdot(stack, G) * (1.0 / (ny * tj))
        m_c, m_n, m_s = mean[0:ti], mean[ti:ti + 1], mean[ti + 8:ti + 9]
        c_own = hdot(f_own, RE) - spread(m_c)
        c_halo = hdot(f_halo, RE)
        m_halo = jnp.concatenate([
            jnp.broadcast_to(m_n, (tj, n)), jnp.broadcast_to(m_s, (tj, n)), m_c, m_c, m_c, m_c,
            jnp.broadcast_to(m_n, (16, n)), jnp.broadcast_to(m_s, (16, n))], axis=0)
        c_halo = jnp.where(valid, c_halo - m_halo, 0.0)
        c_w1, c_w2 = c_halo[o_w:o_w + ti], c_halo[o_w + ti:o_e]
        c_e1, c_e2 = c_halo[o_e:o_e + ti], c_halo[o_e + ti:o_nw]
        c_n, c_s = c_halo[o_n:o_n + tj], c_halo[o_s:o_s + tj]
        c3 = c_own.reshape(ti, tj, n)
        s_own = c_own + 0.25 * (left_of(c_own, c_w1) + right_of(c_own, c_e1))

        def row_smooth(x, lo, hi):
            left = jnp.where(trow == 0, lo, pltpu.roll(x, 1, 0))
            right = jnp.where(trow == tj - 1, hi, pltpu.roll(x, tj - 1, 0))
            return x + 0.25 * (left + right)
        s_n = row_smooth(c_n, c_halo[o_nw:o_nw + 1], c_halo[o_ne:o_ne + 1])
        s_s = row_smooth(c_s, c_halo[o_sw:o_sw + 1], c_halo[o_se:o_se + 1])
        s_w = c_w1 + 0.25 * (c_w2 + c3[:, 0, :])
        s_e = c_e1 + 0.25 * (c3[:, tj - 1, :] + c_e2)
        z_own = f_own + hdot(s_own * cext[0:elems], RF)
        f_rim = jnp.concatenate([f_halo[o_n:o_w], f_halo[o_w:o_w + ti], f_halo[o_e:o_e + ti]], axis=0)
        ok_rim = jnp.concatenate([valid[o_n:o_w], valid[o_w:o_w + ti], valid[o_e:o_e + ti]], axis=0)
        s_rim = jnp.concatenate([s_n, s_s, s_w, s_e], axis=0)
        z_rim = jnp.where(ok_rim, f_rim + hdot(s_rim * cext[elems:elems + h], RF), 0.0)
        return z_own, z_rim

    def operator(z, z_rim):
        nb = [
            jnp.concatenate([z_rim[0:tj], z[0:elems - tj]], axis=0),
            jnp.concatenate([z[tj:], z_rim[tj:2 * tj]], axis=0),
            left_of(z, z_rim[2 * tj:2 * tj + ti]),
            right_of(z, z_rim[2 * tj + ti:2 * tj + 2 * ti]),
        ]
        cols = []
        for f in range(4):
            cols.append((nb[f] * masks[2 * f]).astype(BF16))
            cols.append((nb[f] * masks[2 * f + 1]).astype(BF16))
        lifted = jnp.dot(jnp.concatenate(cols, axis=1), wts[...], preferred_element_type=F32)
        wbuf[...] = lifted.reshape(ti, tj, n)
        erow = iota((tj, n), 0)
        for q in range(0, ti, 2):
            a = z[q * tj:(q + 1) * tj]
            b = z[(q + 1) * tj:(q + 2) * tj]
            lhs = jnp.concatenate([jnp.concatenate(
                [jnp.where(erow == e, a, 0.0), jnp.where(erow == e, b, 0.0)], axis=0).astype(BF16)
                for e in range(tj)], axis=1)
            rhs_w = jnp.concatenate([dvm[q].reshape(tj * n, n), dvm[q + 1].reshape(tj * n, n)], axis=1)
            prod = jnp.dot(lhs, rhs_w, preferred_element_type=F32)
            wbuf[q] += prod[0:tj, 0:n]
            wbuf[q + 1] += prod[tj:2 * tj, n:2 * n]

    bc_wait(0, "recv")
    rim_wait(0, "recv")
    rim_wait(2, "recv")

    cext[elems:elems + h] = chalo[...]
    lens = msgs[0, :, 0, :][:, 0:1]
    start_len = jnp.sqrt(jnp.sum(lens, axis=0, keepdims=True))
    inv_len = 1.0 / start_len
    n_one = lens * inv_len * inv_len
    v1 = rhs2 * inv_len
    v1_halo = jnp.where(valid, halos[0] * inv_len, 0.0)
    lines1 = [p * inv_len for p in three_lines(0)]
    z1, z1_rim = precondition(v1, v1_halo, lines1)
    for c in dcopies:
        c.wait()
    operator(z1, z1_rim)
    fill_sends(1, wbuf)
    start_all(rim_copies(1))
    w1 = wbuf[...].reshape(elems, n)
    own_n1 = total(v1 * v1)
    dot_one = total(v1 * w1)
    p_one = safe_div(dot_one, own_n1)
    gap = w1 - p_one * v1
    msgs[1, me, 0:1] = message([dot_one, p_one, total(gap * gap), own_n1])
    msgs[1, me, 1:2] = packed_rowsum(wbuf[...])
    broadcast(1)
    bc_wait(1, "recv")
    rim_wait(1, "recv")

    X = msgs[1, :, 0, :]
    h11 = jnp.sum(X[:, 0:1], axis=0, keepdims=True)
    dev = X[:, 1:2] - h11
    h21 = jnp.sqrt(jnp.sum(X[:, 2:3] + dev * dev * X[:, 3:4], axis=0, keepdims=True))
    inv21 = 1.0 / h21
    v2 = (w1 - h11 * v1) * inv21
    v2_halo = jnp.where(valid, (halos[1] - h11 * v1_halo) * inv21, 0.0)
    lines2 = [(pw - h11 * pv) * inv21 for pw, pv in zip(three_lines(1), lines1)]
    z2, z2_rim = precondition(v2, v2_halo, lines2)
    operator(z2, z2_rim)
    w2 = wbuf[...].reshape(elems, n)
    alpha = safe_div(total(v1 * v2), own_n1)
    q2 = v2 - alpha * v1
    nq = total(q2 * q2)
    d1 = total(w2 * v1)
    d2 = total(w2 * v2)
    p1 = safe_div(d1, own_n1)
    p2 = safe_div(d2 - alpha * d1, nq)
    gap2 = w2 - p1 * v1 - p2 * q2
    msgs[2, me, 0:1] = message([d1, d2, alpha, nq, p1, p2, total(gap2 * gap2), own_n1])
    msgs[2, me, 1:2] = jnp.zeros((1, n), F32)
    broadcast(2)
    bc_wait(2, "recv")
    Y = msgs[2, :, 0, :]
    h12 = jnp.sum(Y[:, 0:1], axis=0, keepdims=True)
    h22 = jnp.sum(Y[:, 1:2], axis=0, keepdims=True)
    t1 = Y[:, 4:5] - h12 - h22 * Y[:, 2:3]
    t2 = Y[:, 5:6] - h22
    h32 = jnp.sqrt(jnp.sum(t1 * t1 * Y[:, 7:8] + t2 * t2 * Y[:, 3:4] + Y[:, 6:7], axis=0, keepdims=True))

    first = jnp.sqrt(h11 * h11 + h21 * h21)
    cos_one = h11 / first
    sin_one = h21 / first
    upper = cos_one * h12 + sin_one * h22
    lower = -sin_one * h12 + cos_one * h22
    second = jnp.sqrt(lower * lower + h32 * h32)
    cos_two = lower / second
    y2 = cos_two * (-sin_one * start_len) / second
    y1 = (cos_one * start_len - upper * y2) / first
    out[...] = (y1 * z1 + y2 * z2).reshape(ti, tj, n)
    hr, hc = iota((2, 3), 1), iota((2, 3), 0)
    hess_out[...] = jnp.where(
        hr == 0, jnp.where(hc == 0, h11, h12),
        jnp.where(hr == 1, jnp.where(hc == 0, h21, h22), jnp.where(hc == 0, 0.0, h32)))

    for g in range(3):
        bc_wait(g, "send")
        rim_wait(g, "send")


def solution(mesh):
    nx, ny = mesh.shape["gx"], mesh.shape["gy"]

    def body(rhs, diag, lift, state, basis, cinv):
        ti, tj, n = rhs.shape
        kc = basis.shape[1]
        cflat = jnp.transpose(cinv, (0, 2, 3, 1)).reshape(ti, kc * kc, tj)
        sflat = jnp.transpose(state, (0, 2, 1))
        hrows = 2 * tj + 4 * ti + 32
        h = 2 * ti + 2 * tj
        vm = pl.BlockSpec(memory_space=pltpu.VMEM)
        hbm = pl.BlockSpec(memory_space=pltpu.HBM)
        sol, hess = pl.pallas_call(
            functools.partial(kernel, nx, ny, ti, tj, n, kc),
            out_shape=(jax.ShapeDtypeStruct((ti, tj, n), F32), jax.ShapeDtypeStruct((2, 3), F32)),
            in_specs=[hbm] * 6,
            out_specs=(vm, vm),
            scratch_shapes=[
                pltpu.VMEM((ti, tj, n), F32),
                pltpu.VMEM((4, n, n), BF16),
                pltpu.VMEM((ti, 4, tj), jnp.int32),
                pltpu.VMEM((kc, n), F32),
                pltpu.VMEM((ti, kc * kc, tj), F32),
                pltpu.VMEM((ti, tj, n, n), BF16),
                pltpu.VMEM((8 * n, n), BF16),
                pltpu.VMEM((8, ti * tj, n), F32),
                pltpu.VMEM((ti * tj + h, n), F32),
                pltpu.VMEM((ti, tj, n), F32),
                pltpu.VMEM((2, hrows, n), F32),
                pltpu.VMEM((2, hrows, n), F32),
                pltpu.VMEM((h, n), F32),
                pltpu.VMEM((h, n), F32),
                pltpu.VMEM((3, nx * ny, 2, n), F32),
                pltpu.SemaphoreType.DMA((5,)),
                pltpu.SemaphoreType.DMA((ti,)),
                pltpu.SemaphoreType.DMA((3, 8)),
                pltpu.SemaphoreType.DMA((3, 8)),
                pltpu.SemaphoreType.DMA((3,)),
                pltpu.SemaphoreType.DMA((3,)),
            ],
            compiler_params=pltpu.CompilerParams(collective_id=0, has_side_effects=True,
                                                 vmem_limit_bytes=60 * 1024 * 1024),
        )(rhs, diag, lift, sflat, basis.T, cflat)
        return sol, hess.T

    in_specs = (P("gx", "gy", None), P("gx", "gy", None, None), P(), P("gx", "gy", None), P(),
                P("gx", "gy", None, None))
    return jax.shard_map(body, mesh=mesh, in_specs=in_specs, out_specs=(P("gx", "gy", None), P()), check_vma=False)
```

```python
import functools
import jax
import jax.numpy as jnp
from jax import lax
from jax.experimental import pallas as pl
from jax.experimental.pallas import tpu as pltpu
from jax.sharding import PartitionSpec as P

MESH = pl.DeviceIdType.MESH
F32 = jnp.float32
BF16 = jnp.bfloat16


def hdot(a, b, dims=(((1,), (0,)), ((), ()))):
    return lax.dot_general(a, b, dims, precision=lax.Precision.HIGHEST, preferred_element_type=F32)


def total(x):
    return jnp.sum(jnp.sum(x, axis=0, keepdims=True), axis=1, keepdims=True)


def safe_div(a, b):
    return jnp.where(b > 0, a / jnp.where(b > 0, b, 1.0), 0.0)


def iota(shape, dim):
    return lax.broadcasted_iota(jnp.int32, shape, dim)


def kernel(nx, ny, ti, tj, n, kc, rhs_h, diag, lift_h, state_h, basis_h, cinv_h, out, hess_out,
           rhs, lift, state, basis, cinv,
           dvm, wts, masks, cext, wbuf, sends, halos, csend, chalo, msgs,
           isem, dsem, ssem, rsem, msend, mrecv):
    gx = lax.axis_index("gx")
    gy = lax.axis_index("gy")
    me = gx * ny + gy
    count = nx * ny
    elems = ti * tj
    kk = kc * kc

    loads = [pltpu.make_async_copy(a, b, isem.at[q]) for q, (a, b) in enumerate(
        ((rhs_h, rhs), (basis_h, basis), (cinv_h, cinv), (state_h, state), (lift_h, lift)))]
    for c in loads:
        c.start()
    dcopies = [pltpu.make_async_copy(diag.at[q], dvm.at[q], dsem.at[q]) for q in range(ti)]
    for c in dcopies:
        c.start()

    barrier = pltpu.get_barrier_semaphore()

    def greet(k, carry):
        t = lax.rem(me + k, count)
        pl.semaphore_signal(barrier, inc=1, device_id=(t // ny, lax.rem(t, ny)), device_id_type=MESH)
        return carry

    lax.fori_loop(1, count, greet, 0)

    has_n, has_s, has_w, has_e = gx > 0, gx < nx - 1, gy > 0, gy < ny - 1
    h = 2 * ti + 2 * tj
    o_n, o_s, o_w, o_e = 0, tj, 2 * tj, 2 * tj + 2 * ti
    o_nw = 2 * tj + 4 * ti
    o_ne, o_sw, o_se = o_nw + 8, o_nw + 16, o_nw + 24
    hrows = o_nw + 32
    routes = [
        (has_n, (gx - 1, gy), o_n, o_s, tj),
        (has_s, (gx + 1, gy), o_s, o_n, tj),
        (has_w, (gx, gy - 1), o_w, o_e, 2 * ti),
        (has_e, (gx, gy + 1), o_e, o_w, 2 * ti),
        (jnp.logical_and(has_n, has_w), (gx - 1, gy - 1), o_nw, o_se, 8),
        (jnp.logical_and(has_n, has_e), (gx - 1, gy + 1), o_ne, o_sw, 8),
        (jnp.logical_and(has_s, has_w), (gx + 1, gy - 1), o_sw, o_ne, 8),
        (jnp.logical_and(has_s, has_e), (gx + 1, gy + 1), o_se, o_nw, 8),
    ]
    croutes = [
        (has_n, (gx - 1, gy), 0, tj, tj),
        (has_s, (gx + 1, gy), tj, 0, tj),
        (has_w, (gx, gy - 1), 2 * tj, 2 * tj + ti, ti),
        (has_e, (gx, gy + 1), 2 * tj + ti, 2 * tj, ti),
    ]
    opposite = [1, 0, 3, 2, 7, 6, 5, 4]

    def rim_copies(g):
        return [(ok, pltpu.make_async_remote_copy(
            src_ref=sends.at[g, pl.ds(src, rows)], dst_ref=halos.at[g, pl.ds(dst, rows)],
            send_sem=ssem.at[g, d], recv_sem=rsem.at[g, opposite[d]],
            device_id=dev, device_id_type=MESH)) for d, (ok, dev, src, dst, rows) in enumerate(routes)]

    def coarse_copies():
        return [(ok, pltpu.make_async_remote_copy(
            src_ref=csend.at[pl.ds(src, rows)], dst_ref=chalo.at[pl.ds(dst, rows)],
            send_sem=ssem.at[2, d], recv_sem=rsem.at[2, opposite[d]],
            device_id=dev, device_id_type=MESH)) for d, (ok, dev, src, dst, rows) in enumerate(croutes)]

    def rim_wait(g, which):
        table = routes if g < 2 else croutes
        for d, (ok, dev, src, dst, rows) in enumerate(table):
            @pl.when(ok)
            def _(d=d, dev=dev, src=src, rows=rows):
                if g < 2:
                    s, r = sends.at[g, pl.ds(src, rows)], halos.at[g, pl.ds(src, rows)]
                else:
                    s, r = csend.at[pl.ds(src, rows)], chalo.at[pl.ds(src, rows)]
                c = pltpu.make_async_remote_copy(
                    src_ref=s, dst_ref=r, send_sem=ssem.at[g, d], recv_sem=rsem.at[g, d],
                    device_id=dev, device_id_type=MESH)
                if which == "send":
                    c.wait_send()
                else:
                    c.wait_recv()

    def start_all(copies):
        for ok, c in copies:
            @pl.when(ok)
            def _(c=c):
                c.start()

    def broadcast(g):
        def one(k, carry):
            t = lax.rem(me + k, count)
            pltpu.make_async_remote_copy(
                src_ref=msgs.at[g, me], dst_ref=msgs.at[g, me], send_sem=msend.at[g], recv_sem=mrecv.at[g],
                device_id=(t // ny, lax.rem(t, ny)), device_id_type=MESH).start()
            return carry
        lax.fori_loop(1, count, one, 0)

    def bc_wait(g, which):
        part = msgs.at[g, pl.ds(0, count - 1)]
        c = pltpu.make_async_remote_copy(
            src_ref=part, dst_ref=part, send_sem=msend.at[g], recv_sem=mrecv.at[g],
            device_id=(gx, gy), device_id_type=MESH)
        if which == "send":
            c.wait_send()
        else:
            c.wait_recv()

    def fill_sends(g, ref):
        sends[g, o_n:o_n + tj] = ref[0]
        sends[g, o_s:o_s + tj] = ref[ti - 1]
        sends[g, o_w:o_w + ti] = ref[:, 0, :]
        sends[g, o_w + ti:o_w + 2 * ti] = ref[:, 1, :]
        sends[g, o_e:o_e + ti] = ref[:, tj - 1, :]
        sends[g, o_e + ti:o_e + 2 * ti] = ref[:, tj - 2, :]
        sends[g, o_nw:o_nw + 8] = jnp.broadcast_to(ref[0, 0:1, :], (8, n))
        sends[g, o_ne:o_ne + 8] = jnp.broadcast_to(ref[0, tj - 1:tj, :], (8, n))
        sends[g, o_sw:o_sw + 8] = jnp.broadcast_to(ref[ti - 1, 0:1, :], (8, n))
        sends[g, o_se:o_se + 8] = jnp.broadcast_to(ref[ti - 1, tj - 1:tj, :], (8, n))

    lane1 = iota((1, n), 1)

    def message(values):
        row = jnp.zeros((1, n), F32)
        for p, v in enumerate(values):
            row = jnp.where(lane1 == p, v, row)
        return row

    e1 = (iota((kc, n), 1) // kc == iota((kc, n), 0)).astype(F32)
    e3 = (lax.rem(iota((kc, n), 1), kc) == iota((kc, n), 0)).astype(F32)
    pick = iota((ti, n), 1) // kc == iota((ti, n), 0)
    loads[0].wait()
    loads[1].wait()
    Rt = basis[...]
    over_first = (((0,), (0,)), ((), ()))
    RT = hdot(Rt, e3, over_first)

    def packed_rowsum(f3):
        rows = hdot(jnp.sum(f3, axis=1), RT)
        return jnp.sum(jnp.where(pick, rows, 0.0), axis=0, keepdims=True)

    rhs3 = rhs[...]
    rhs2 = rhs3.reshape(elems, n)
    fill_sends(0, rhs)
    msgs[0, me, 0:1] = message([total(rhs2 * rhs2)])
    msgs[0, me, 1:2] = packed_rowsum(rhs3)

    pl.semaphore_wait(barrier, count - 1)
    broadcast(0)
    start_all(rim_copies(0))
    loads[2].wait()
    cext[...] = jnp.zeros_like(cext)
    eye = (iota((tj, tj), 0) == iota((tj, tj), 1)).astype(F32)
    for q in range(ti):
        cext[q * tj:(q + 1) * tj, 0:kk] = hdot(eye, cinv[q], (((1,), (1,)), ((), ())))
    c3d = cext[0:elems].reshape(ti, tj, n)
    csend[0:tj] = c3d[0]
    csend[tj:2 * tj] = c3d[ti - 1]
    csend[2 * tj:2 * tj + ti] = c3d[:, 0, :]
    csend[2 * tj + ti:2 * tj + 2 * ti] = c3d[:, tj - 1, :]
    start_all(coarse_copies())

    RE = hdot(Rt, e1, over_first)
    e4 = (lax.rem(iota((n, kc), 0), kc) == iota((n, kc), 1)).astype(F32)
    RF = hdot(e4, Rt)
    G = (lax.rem(iota((n, n), 0), kc) == iota((n, n), 1) // kc).astype(F32)
    flip = (iota((n, n), 0) + iota((n, n), 1) == n - 1).astype(BF16)
    loads[4].wait()
    for f in range(4):
        wts[2 * f * n:(2 * f + 1) * n] = lift[f]
        wts[(2 * f + 1) * n:(2 * f + 2) * n] = jnp.dot(flip, lift[f], preferred_element_type=F32).astype(BF16)
    loads[3].wait()
    own_j = lax.rem(iota((elems, tj), 0), tj) == iota((elems, tj), 1)
    ones = jnp.ones((tj, n), BF16)
    for f in range(4):
        rows = state[:, f, :].astype(F32)
        wide = jnp.broadcast_to(rows[:, None, :], (ti, tj, tj)).reshape(elems, tj)
        col = jnp.dot(jnp.where(own_j, wide, 0.0).astype(BF16), ones, preferred_element_type=F32)
        masks[2 * f] = (col == 1.0).astype(F32)
        masks[2 * f + 1] = (col == 2.0).astype(F32)

    hrow = iota((hrows, 1), 0)
    n_i, s_i, w_i, e_i = [v.astype(jnp.int32) for v in (has_n, has_s, has_w, has_e)]
    valid = jnp.where(hrow < o_s, n_i, jnp.where(hrow < o_w, s_i, jnp.where(
        hrow < o_e, w_i, jnp.where(hrow < o_nw, e_i, jnp.where(
            hrow < o_ne, n_i * w_i, jnp.where(hrow < o_sw, n_i * e_i, jnp.where(
                hrow < o_se, s_i * w_i, s_i * e_i))))))) > 0

    jrow = lax.rem(iota((elems, 1), 0), tj)
    trow = iota((tj, 1), 0)

    def spread(col):
        return jnp.broadcast_to(col[:, None, :], (ti, tj, n)).reshape(elems, n)

    def left_of(x, edge):
        return jnp.where(jrow == 0, spread(edge), pltpu.roll(x, 1, 0))

    def right_of(x, edge):
        return jnp.where(jrow == tj - 1, spread(edge), pltpu.roll(x, elems - 1, 0))

    def line_sum(g, line):
        acc = msgs[g, line * ny, 1:2]
        for q in range(1, ny):
            acc = acc + msgs[g, line * ny + q, 1:2]
        return acc

    def three_lines(g):
        return (line_sum(g, gx), line_sum(g, jnp.maximum(gx - 1, 0)), line_sum(g, jnp.minimum(gx + 1, nx - 1)))

    def precondition(f_own, f_halo, lines, coarse):
        p_c, p_n, p_s = lines
        stack = jnp.concatenate([
            jnp.where(pick, jnp.broadcast_to(p_c, (ti, n)), 0.0),
            jnp.broadcast_to(jnp.where(lane1 // kc == ti - 1, p_n, 0.0), (8, n)),
            jnp.broadcast_to(jnp.where(lane1 // kc == 0, p_s, 0.0), (8, n))], axis=0)
        mean = hdot(stack, G) * (1.0 / (ny * tj))
        m_c, m_n, m_s = mean[0:ti], mean[ti:ti + 1], mean[ti + 8:ti + 9]
        c_own = coarse - spread(m_c)
        c_halo = hdot(f_halo, RE)
        m_halo = jnp.concatenate([
            jnp.broadcast_to(m_n, (tj, n)), jnp.broadcast_to(m_s, (tj, n)), m_c, m_c, m_c, m_c,
            jnp.broadcast_to(m_n, (16, n)), jnp.broadcast_to(m_s, (16, n))], axis=0)
        c_halo = jnp.where(valid, c_halo - m_halo, 0.0)
        c_w1, c_w2 = c_halo[o_w:o_w + ti], c_halo[o_w + ti:o_e]
        c_e1, c_e2 = c_halo[o_e:o_e + ti], c_halo[o_e + ti:o_nw]
        c_n, c_s = c_halo[o_n:o_n + tj], c_halo[o_s:o_s + tj]
        c3 = c_own.reshape(ti, tj, n)
        s_own = c_own + 0.25 * (left_of(c_own, c_w1) + right_of(c_own, c_e1))

        def row_smooth(x, lo, hi):
            left = jnp.where(trow == 0, lo, pltpu.roll(x, 1, 0))
            right = jnp.where(trow == tj - 1, hi, pltpu.roll(x, tj - 1, 0))
            return x + 0.25 * (left + right)
        s_n = row_smooth(c_n, c_halo[o_nw:o_nw + 1], c_halo[o_ne:o_ne + 1])
        s_s = row_smooth(c_s, c_halo[o_sw:o_sw + 1], c_halo[o_se:o_se + 1])
        s_w = c_w1 + 0.25 * (c_w2 + c3[:, 0, :])
        s_e = c_e1 + 0.25 * (c3[:, tj - 1, :] + c_e2)
        z_own = f_own + hdot(s_own * cext[0:elems], RF)
        f_rim = jnp.concatenate([f_halo[o_n:o_w], f_halo[o_w:o_w + ti], f_halo[o_e:o_e + ti]], axis=0)
        ok_rim = jnp.concatenate([valid[o_n:o_w], valid[o_w:o_w + ti], valid[o_e:o_e + ti]], axis=0)
        s_rim = jnp.concatenate([s_n, s_s, s_w, s_e], axis=0)
        z_rim = jnp.where(ok_rim, f_rim + hdot(s_rim * cext[elems:elems + h], RF), 0.0)
        return z_own, z_rim

    def operator(z, z_rim):
        nb = [
            jnp.concatenate([z_rim[0:tj], z[0:elems - tj]], axis=0),
            jnp.concatenate([z[tj:], z_rim[tj:2 * tj]], axis=0),
            left_of(z, z_rim[2 * tj:2 * tj + ti]),
            right_of(z, z_rim[2 * tj + ti:2 * tj + 2 * ti]),
        ]
        cols = []
        for f in range(4):
            cols.append((nb[f] * masks[2 * f]).astype(BF16))
            cols.append((nb[f] * masks[2 * f + 1]).astype(BF16))
        lifted = jnp.dot(jnp.concatenate(cols, axis=1), wts[...], preferred_element_type=F32)
        wbuf[...] = lifted.reshape(ti, tj, n)
        erow = iota((tj, n), 0)
        for q in range(0, ti, 2):
            a = z[q * tj:(q + 1) * tj]
            b = z[(q + 1) * tj:(q + 2) * tj]
            lhs = jnp.concatenate([jnp.concatenate(
                [jnp.where(erow == e, a, 0.0), jnp.where(erow == e, b, 0.0)], axis=0).astype(BF16)
                for e in range(tj)], axis=1)
            rhs_w = jnp.concatenate([dvm[q].reshape(tj * n, n), dvm[q + 1].reshape(tj * n, n)], axis=1)
            prod = jnp.dot(lhs, rhs_w, preferred_element_type=F32)
            wbuf[q] += prod[0:tj, 0:n]
            wbuf[q + 1] += prod[tj:2 * tj, n:2 * n]

    coarse_rhs = hdot(rhs2, RE)
    bc_wait(0, "recv")
    rim_wait(0, "recv")
    rim_wait(2, "recv")

    cext[elems:elems + h] = chalo[...]
    lens = msgs[0, :, 0, :][:, 0:1]
    start_len = jnp.sqrt(jnp.sum(lens, axis=0, keepdims=True))
    inv_len = 1.0 / start_len
    n_one = lens * inv_len * inv_len
    v1 = rhs2 * inv_len
    v1_halo = jnp.where(valid, halos[0] * inv_len, 0.0)
    lines1 = [p * inv_len for p in three_lines(0)]
    coarse1 = coarse_rhs * inv_len
    z1, z1_rim = precondition(v1, v1_halo, lines1, coarse1)
    for c in dcopies:
        c.wait()
    operator(z1, z1_rim)
    fill_sends(1, wbuf)
    start_all(rim_copies(1))
    w1 = wbuf[...].reshape(elems, n)
    own_n1 = total(v1 * v1)
    dot_one = total(v1 * w1)
    p_one = safe_div(dot_one, own_n1)
    gap = w1 - p_one * v1
    msgs[1, me, 0:1] = message([dot_one, p_one, total(gap * gap), own_n1])
    msgs[1, me, 1:2] = packed_rowsum(wbuf[...])
    broadcast(1)
    coarse_w = hdot(w1, RE)
    bc_wait(1, "recv")
    rim_wait(1, "recv")

    X = msgs[1, :, 0, :]
    h11 = jnp.sum(X[:, 0:1], axis=0, keepdims=True)
    dev = X[:, 1:2] - h11
    h21 = jnp.sqrt(jnp.sum(X[:, 2:3] + dev * dev * X[:, 3:4], axis=0, keepdims=True))
    inv21 = 1.0 / h21
    v2 = (w1 - h11 * v1) * inv21
    v2_halo = jnp.where(valid, (halos[1] - h11 * v1_halo) * inv21, 0.0)
    lines2 = [(pw - h11 * pv) * inv21 for pw, pv in zip(three_lines(1), lines1)]
    z2, z2_rim = precondition(v2, v2_halo, lines2, (coarse_w - h11 * coarse1) * inv21)
    operator(z2, z2_rim)
    w2 = wbuf[...].reshape(elems, n)
    alpha = safe_div(total(v1 * v2), own_n1)
    q2 = v2 - alpha * v1
    nq = total(q2 * q2)
    d1 = total(w2 * v1)
    d2 = total(w2 * v2)
    p1 = safe_div(d1, own_n1)
    p2 = safe_div(d2 - alpha * d1, nq)
    gap2 = w2 - p1 * v1 - p2 * q2
    msgs[2, me, 0:1] = message([d1, d2, alpha, nq, p1, p2, total(gap2 * gap2), own_n1])
    msgs[2, me, 1:2] = jnp.zeros((1, n), F32)
    broadcast(2)
    bc_wait(2, "recv")
    Y = msgs[2, :, 0, :]
    h12 = jnp.sum(Y[:, 0:1], axis=0, keepdims=True)
    h22 = jnp.sum(Y[:, 1:2], axis=0, keepdims=True)
    t1 = Y[:, 4:5] - h12 - h22 * Y[:, 2:3]
    t2 = Y[:, 5:6] - h22
    h32 = jnp.sqrt(jnp.sum(t1 * t1 * Y[:, 7:8] + t2 * t2 * Y[:, 3:4] + Y[:, 6:7], axis=0, keepdims=True))

    first = jnp.sqrt(h11 * h11 + h21 * h21)
    cos_one = h11 / first
    sin_one = h21 / first
    upper = cos_one * h12 + sin_one * h22
    lower = -sin_one * h12 + cos_one * h22
    second = jnp.sqrt(lower * lower + h32 * h32)
    cos_two = lower / second
    y2 = cos_two * (-sin_one * start_len) / second
    y1 = (cos_one * start_len - upper * y2) / first
    out[...] = (y1 * z1 + y2 * z2).reshape(ti, tj, n)
    hr, hc = iota((2, 3), 1), iota((2, 3), 0)
    hess_out[...] = jnp.where(
        hr == 0, jnp.where(hc == 0, h11, h12),
        jnp.where(hr == 1, jnp.where(hc == 0, h21, h22), jnp.where(hc == 0, 0.0, h32)))

    for g in range(3):
        bc_wait(g, "send")
        rim_wait(g, "send")


def hand_on(sol_in, hess_in, sol_out, hess_out):
    sol_out[...] = sol_in[...]
    hess_out[...] = hess_in[...]


def solution(mesh):
    nx, ny = mesh.shape["gx"], mesh.shape["gy"]

    def body(rhs, diag, lift, state, basis, cinv):
        ti, tj, n = rhs.shape
        kc = basis.shape[1]
        cflat = jnp.transpose(cinv, (0, 2, 3, 1)).reshape(ti, kc * kc, tj)
        sflat = jnp.transpose(state, (0, 2, 1))
        hrows = 2 * tj + 4 * ti + 32
        h = 2 * ti + 2 * tj
        vm = pl.BlockSpec(memory_space=pltpu.VMEM)
        hbm = pl.BlockSpec(memory_space=pltpu.HBM)
        sol, hess = pl.pallas_call(
            functools.partial(kernel, nx, ny, ti, tj, n, kc),
            out_shape=(jax.ShapeDtypeStruct((ti, tj, n), F32), jax.ShapeDtypeStruct((2, 3), F32)),
            in_specs=[hbm] * 6,
            out_specs=(vm, vm),
            scratch_shapes=[
                pltpu.VMEM((ti, tj, n), F32),
                pltpu.VMEM((4, n, n), BF16),
                pltpu.VMEM((ti, 4, tj), jnp.int32),
                pltpu.VMEM((kc, n), F32),
                pltpu.VMEM((ti, kc * kc, tj), F32),
                pltpu.VMEM((ti, tj, n, n), BF16),
                pltpu.VMEM((8 * n, n), BF16),
                pltpu.VMEM((8, ti * tj, n), F32),
                pltpu.VMEM((ti * tj + h, n), F32),
                pltpu.VMEM((ti, tj, n), F32),
                pltpu.VMEM((2, hrows, n), F32),
                pltpu.VMEM((2, hrows, n), F32),
                pltpu.VMEM((h, n), F32),
                pltpu.VMEM((h, n), F32),
                pltpu.VMEM((3, nx * ny, 2, n), F32),
                pltpu.SemaphoreType.DMA((5,)),
                pltpu.SemaphoreType.DMA((ti,)),
                pltpu.SemaphoreType.DMA((3, 8)),
                pltpu.SemaphoreType.DMA((3, 8)),
                pltpu.SemaphoreType.DMA((3,)),
                pltpu.SemaphoreType.DMA((3,)),
            ],
            compiler_params=pltpu.CompilerParams(collective_id=0, has_side_effects=True,
                                                 vmem_limit_bytes=60 * 1024 * 1024),
        )(rhs, diag, lift, sflat, basis.T, cflat)
        sol, hess = pl.pallas_call(
            hand_on,
            out_shape=(jax.ShapeDtypeStruct(sol.shape, F32), jax.ShapeDtypeStruct(hess.shape, F32)),
            in_specs=[vm, vm],
            out_specs=(vm, vm),
            compiler_params=pltpu.CompilerParams(vmem_limit_bytes=60 * 1024 * 1024),
        )(sol, hess)
        return sol, hess.T

    in_specs = (P("gx", "gy", None), P("gx", "gy", None, None), P(), P("gx", "gy", None), P(),
                P("gx", "gy", None, None))
    return jax.shard_map(body, mesh=mesh, in_specs=in_specs, out_specs=(P("gx", "gy", None), P()), check_vma=False)
```

```python
import functools
import jax
import jax.numpy as jnp
from jax import lax
from jax.experimental import pallas as pl
from jax.experimental.pallas import tpu as pltpu
from jax.sharding import PartitionSpec as P

MESH = pl.DeviceIdType.MESH
F32 = jnp.float32
BF16 = jnp.bfloat16


def hdot(a, b, dims=(((1,), (0,)), ((), ()))):
    return lax.dot_general(a, b, dims, precision=lax.Precision.HIGHEST, preferred_element_type=F32)


def total(x):
    return jnp.sum(jnp.sum(x, axis=0, keepdims=True), axis=1, keepdims=True)


def safe_div(a, b):
    return jnp.where(b > 0, a / jnp.where(b > 0, b, 1.0), 0.0)


def iota(shape, dim):
    return lax.broadcasted_iota(jnp.int32, shape, dim)


def kernel(nx, ny, ti, tj, n, kc, rhs_h, diag, lift_h, state_h, basis_h, cinv_h, out, hess_out,
           rhs, lift, state, basis, cinv,
           dvm, wts, masks, cext, wbuf, sends, halos, csend, chalo, msgs,
           isem, dsem, ssem, rsem, msend, mrecv):
    gx = lax.axis_index("gx")
    gy = lax.axis_index("gy")
    me = gx * ny + gy
    count = nx * ny
    elems = ti * tj
    kk = kc * kc

    barrier = pltpu.get_barrier_semaphore()

    def greet(k, carry):
        t = lax.rem(me + k, count)
        pl.semaphore_signal(barrier, inc=1, device_id=(t // ny, lax.rem(t, ny)), device_id_type=MESH)
        return carry

    lax.fori_loop(1, count, greet, 0)

    loads = [pltpu.make_async_copy(a, b, isem.at[q]) for q, (a, b) in enumerate(
        ((rhs_h, rhs), (basis_h, basis), (cinv_h, cinv), (state_h, state), (lift_h, lift)))]
    for c in loads:
        c.start()
    dcopies = [pltpu.make_async_copy(diag.at[q], dvm.at[q], dsem.at[q]) for q in range(ti)]
    for c in dcopies:
        c.start()

    has_n, has_s, has_w, has_e = gx > 0, gx < nx - 1, gy > 0, gy < ny - 1
    h = 2 * ti + 2 * tj
    o_n, o_s, o_w, o_e = 0, tj, 2 * tj, 2 * tj + 2 * ti
    o_nw = 2 * tj + 4 * ti
    o_ne, o_sw, o_se = o_nw + 8, o_nw + 16, o_nw + 24
    hrows = o_nw + 32
    routes = [
        (has_n, (gx - 1, gy), o_n, o_s, tj),
        (has_s, (gx + 1, gy), o_s, o_n, tj),
        (has_w, (gx, gy - 1), o_w, o_e, 2 * ti),
        (has_e, (gx, gy + 1), o_e, o_w, 2 * ti),
        (jnp.logical_and(has_n, has_w), (gx - 1, gy - 1), o_nw, o_se, 8),
        (jnp.logical_and(has_n, has_e), (gx - 1, gy + 1), o_ne, o_sw, 8),
        (jnp.logical_and(has_s, has_w), (gx + 1, gy - 1), o_sw, o_ne, 8),
        (jnp.logical_and(has_s, has_e), (gx + 1, gy + 1), o_se, o_nw, 8),
    ]
    croutes = [
        (has_n, (gx - 1, gy), 0, tj, tj),
        (has_s, (gx + 1, gy), tj, 0, tj),
        (has_w, (gx, gy - 1), 2 * tj, 2 * tj + ti, ti),
        (has_e, (gx, gy + 1), 2 * tj + ti, 2 * tj, ti),
    ]
    opposite = [1, 0, 3, 2, 7, 6, 5, 4]

    def rim_copies(g):
        return [(ok, pltpu.make_async_remote_copy(
            src_ref=sends.at[g, pl.ds(src, rows)], dst_ref=halos.at[g, pl.ds(dst, rows)],
            send_sem=ssem.at[g, d], recv_sem=rsem.at[g, opposite[d]],
            device_id=dev, device_id_type=MESH)) for d, (ok, dev, src, dst, rows) in enumerate(routes)]

    def coarse_copies():
        return [(ok, pltpu.make_async_remote_copy(
            src_ref=csend.at[pl.ds(src, rows)], dst_ref=chalo.at[pl.ds(dst, rows)],
            send_sem=ssem.at[2, d], recv_sem=rsem.at[2, opposite[d]],
            device_id=dev, device_id_type=MESH)) for d, (ok, dev, src, dst, rows) in enumerate(croutes)]

    def rim_wait(g, which):
        table = routes if g < 2 else croutes
        for d, (ok, dev, src, dst, rows) in enumerate(table):
            @pl.when(ok)
            def _(d=d, dev=dev, src=src, rows=rows):
                if g < 2:
                    s, r = sends.at[g, pl.ds(src, rows)], halos.at[g, pl.ds(src, rows)]
                else:
                    s, r = csend.at[pl.ds(src, rows)], chalo.at[pl.ds(src, rows)]
                c = pltpu.make_async_remote_copy(
                    src_ref=s, dst_ref=r, send_sem=ssem.at[g, d], recv_sem=rsem.at[g, d],
                    device_id=dev, device_id_type=MESH)
                if which == "send":
                    c.wait_send()
                else:
                    c.wait_recv()

    def start_all(copies):
        for ok, c in copies:
            @pl.when(ok)
            def _(c=c):
                c.start()

    def broadcast(g):
        def one(k, carry):
            t = lax.rem(me + k, count)
            pltpu.make_async_remote_copy(
                src_ref=msgs.at[g, me], dst_ref=msgs.at[g, me], send_sem=msend.at[g], recv_sem=mrecv.at[g],
                device_id=(t // ny, lax.rem(t, ny)), device_id_type=MESH).start()
            return carry
        lax.fori_loop(1, count, one, 0)

    def bc_wait(g, which):
        part = msgs.at[g, pl.ds(0, count - 1)]
        c = pltpu.make_async_remote_copy(
            src_ref=part, dst_ref=part, send_sem=msend.at[g], recv_sem=mrecv.at[g],
            device_id=(gx, gy), device_id_type=MESH)
        if which == "send":
            c.wait_send()
        else:
            c.wait_recv()

    def fill_sends(g, ref):
        sends[g, o_n:o_n + tj] = ref[0]
        sends[g, o_s:o_s + tj] = ref[ti - 1]
        sends[g, o_w:o_w + ti] = ref[:, 0, :]
        sends[g, o_w + ti:o_w + 2 * ti] = ref[:, 1, :]
        sends[g, o_e:o_e + ti] = ref[:, tj - 1, :]
        sends[g, o_e + ti:o_e + 2 * ti] = ref[:, tj - 2, :]
        sends[g, o_nw:o_nw + 8] = jnp.broadcast_to(ref[0, 0:1, :], (8, n))
        sends[g, o_ne:o_ne + 8] = jnp.broadcast_to(ref[0, tj - 1:tj, :], (8, n))
        sends[g, o_sw:o_sw + 8] = jnp.broadcast_to(ref[ti - 1, 0:1, :], (8, n))
        sends[g, o_se:o_se + 8] = jnp.broadcast_to(ref[ti - 1, tj - 1:tj, :], (8, n))

    lane1 = iota((1, n), 1)

    def message(values):
        row = jnp.zeros((1, n), F32)
        for p, v in enumerate(values):
            row = jnp.where(lane1 == p, v, row)
        return row

    e1 = (iota((kc, n), 1) // kc == iota((kc, n), 0)).astype(F32)
    e3 = (lax.rem(iota((kc, n), 1), kc) == iota((kc, n), 0)).astype(F32)
    pick = iota((ti, n), 1) // kc == iota((ti, n), 0)
    loads[0].wait()
    loads[1].wait()
    Rt = basis[...]
    over_first = (((0,), (0,)), ((), ()))
    RT = hdot(Rt, e3, over_first)

    def packed_rowsum(f3):
        rows = hdot(jnp.sum(f3, axis=1), RT)
        return jnp.sum(jnp.where(pick, rows, 0.0), axis=0, keepdims=True)

    rhs3 = rhs[...]
    rhs2 = rhs3.reshape(elems, n)
    fill_sends(0, rhs)
    msgs[0, me, 0:1] = message([total(rhs2 * rhs2)])
    msgs[0, me, 1:2] = packed_rowsum(rhs3)

    loads[2].wait()
    cext[...] = jnp.zeros_like(cext)
    eye = (iota((tj, tj), 0) == iota((tj, tj), 1)).astype(F32)
    for q in range(ti):
        cext[q * tj:(q + 1) * tj, 0:kk] = hdot(eye, cinv[q], (((1,), (1,)), ((), ())))
    c3d = cext[0:elems].reshape(ti, tj, n)
    csend[0:tj] = c3d[0]
    csend[tj:2 * tj] = c3d[ti - 1]
    csend[2 * tj:2 * tj + ti] = c3d[:, 0, :]
    csend[2 * tj + ti:2 * tj + 2 * ti] = c3d[:, tj - 1, :]
    pl.semaphore_wait(barrier, count - 1)
    broadcast(0)
    start_all(rim_copies(0))
    start_all(coarse_copies())

    RE = hdot(Rt, e1, over_first)
    e4 = (lax.rem(iota((n, kc), 0), kc) == iota((n, kc), 1)).astype(F32)
    RF = hdot(e4, Rt)
    G = (lax.rem(iota((n, n), 0), kc) == iota((n, n), 1) // kc).astype(F32)
    flip = (iota((n, n), 0) + iota((n, n), 1) == n - 1).astype(BF16)
    loads[4].wait()
    for f in range(4):
        wts[2 * f * n:(2 * f + 1) * n] = lift[f]
        wts[(2 * f + 1) * n:(2 * f + 2) * n] = jnp.dot(flip, lift[f], preferred_element_type=F32).astype(BF16)
    loads[3].wait()
    own_j = lax.rem(iota((elems, tj), 0), tj) == iota((elems, tj), 1)
    ones = jnp.ones((tj, n), BF16)
    for f in range(4):
        rows = state[:, f, :].astype(F32)
        wide = jnp.broadcast_to(rows[:, None, :], (ti, tj, tj)).reshape(elems, tj)
        col = jnp.dot(jnp.where(own_j, wide, 0.0).astype(BF16), ones, preferred_element_type=F32)
        masks[2 * f] = (col == 1.0).astype(F32)
        masks[2 * f + 1] = (col == 2.0).astype(F32)

    hrow = iota((hrows, 1), 0)
    n_i, s_i, w_i, e_i = [v.astype(jnp.int32) for v in (has_n, has_s, has_w, has_e)]
    valid = jnp.where(hrow < o_s, n_i, jnp.where(hrow < o_w, s_i, jnp.where(
        hrow < o_e, w_i, jnp.where(hrow < o_nw, e_i, jnp.where(
            hrow < o_ne, n_i * w_i, jnp.where(hrow < o_sw, n_i * e_i, jnp.where(
                hrow < o_se, s_i * w_i, s_i * e_i))))))) > 0

    jrow = lax.rem(iota((elems, 1), 0), tj)
    trow = iota((tj, 1), 0)

    def spread(col):
        return jnp.broadcast_to(col[:, None, :], (ti, tj, n)).reshape(elems, n)

    def left_of(x, edge):
        return jnp.where(jrow == 0, spread(edge), pltpu.roll(x, 1, 0))

    def right_of(x, edge):
        return jnp.where(jrow == tj - 1, spread(edge), pltpu.roll(x, elems - 1, 0))

    def line_sum(g, line):
        acc = msgs[g, line * ny, 1:2]
        for q in range(1, ny):
            acc = acc + msgs[g, line * ny + q, 1:2]
        return acc

    def three_lines(g):
        return (line_sum(g, gx), line_sum(g, jnp.maximum(gx - 1, 0)), line_sum(g, jnp.minimum(gx + 1, nx - 1)))

    def precondition(f_own, f_halo, lines, coarse):
        p_c, p_n, p_s = lines
        stack = jnp.concatenate([
            jnp.where(pick, jnp.broadcast_to(p_c, (ti, n)), 0.0),
            jnp.broadcast_to(jnp.where(lane1 // kc == ti - 1, p_n, 0.0), (8, n)),
            jnp.broadcast_to(jnp.where(lane1 // kc == 0, p_s, 0.0), (8, n))], axis=0)
        mean = hdot(stack, G) * (1.0 / (ny * tj))
        m_c, m_n, m_s = mean[0:ti], mean[ti:ti + 1], mean[ti + 8:ti + 9]
        c_own = coarse - spread(m_c)
        c_halo = hdot(f_halo, RE)
        m_halo = jnp.concatenate([
            jnp.broadcast_to(m_n, (tj, n)), jnp.broadcast_to(m_s, (tj, n)), m_c, m_c, m_c, m_c,
            jnp.broadcast_to(m_n, (16, n)), jnp.broadcast_to(m_s, (16, n))], axis=0)
        c_halo = jnp.where(valid, c_halo - m_halo, 0.0)
        c_w1, c_w2 = c_halo[o_w:o_w + ti], c_halo[o_w + ti:o_e]
        c_e1, c_e2 = c_halo[o_e:o_e + ti], c_halo[o_e + ti:o_nw]
        c_n, c_s = c_halo[o_n:o_n + tj], c_halo[o_s:o_s + tj]
        c3 = c_own.reshape(ti, tj, n)
        s_own = c_own + 0.25 * (left_of(c_own, c_w1) + right_of(c_own, c_e1))

        def row_smooth(x, lo, hi):
            left = jnp.where(trow == 0, lo, pltpu.roll(x, 1, 0))
            right = jnp.where(trow == tj - 1, hi, pltpu.roll(x, tj - 1, 0))
            return x + 0.25 * (left + right)
        s_n = row_smooth(c_n, c_halo[o_nw:o_nw + 1], c_halo[o_ne:o_ne + 1])
        s_s = row_smooth(c_s, c_halo[o_sw:o_sw + 1], c_halo[o_se:o_se + 1])
        s_w = c_w1 + 0.25 * (c_w2 + c3[:, 0, :])
        s_e = c_e1 + 0.25 * (c3[:, tj - 1, :] + c_e2)
        z_own = f_own + hdot(s_own * cext[0:elems], RF)
        f_rim = jnp.concatenate([f_halo[o_n:o_w], f_halo[o_w:o_w + ti], f_halo[o_e:o_e + ti]], axis=0)
        ok_rim = jnp.concatenate([valid[o_n:o_w], valid[o_w:o_w + ti], valid[o_e:o_e + ti]], axis=0)
        s_rim = jnp.concatenate([s_n, s_s, s_w, s_e], axis=0)
        z_rim = jnp.where(ok_rim, f_rim + hdot(s_rim * cext[elems:elems + h], RF), 0.0)
        return z_own, z_rim

    def operator(z, z_rim):
        nb = [
            jnp.concatenate([z_rim[0:tj], z[0:elems - tj]], axis=0),
            jnp.concatenate([z[tj:], z_rim[tj:2 * tj]], axis=0),
            left_of(z, z_rim[2 * tj:2 * tj + ti]),
            right_of(z, z_rim[2 * tj + ti:2 * tj + 2 * ti]),
        ]
        cols = []
        for f in range(4):
            cols.append((nb[f] * masks[2 * f]).astype(BF16))
            cols.append((nb[f] * masks[2 * f + 1]).astype(BF16))
        lifted = jnp.dot(jnp.concatenate(cols, axis=1), wts[...], preferred_element_type=F32)
        wbuf[...] = lifted.reshape(ti, tj, n)
        erow = iota((tj, n), 0)
        for q in range(0, ti, 2):
            a = z[q * tj:(q + 1) * tj]
            b = z[(q + 1) * tj:(q + 2) * tj]
            lhs = jnp.concatenate([jnp.concatenate(
                [jnp.where(erow == e, a, 0.0), jnp.where(erow == e, b, 0.0)], axis=0).astype(BF16)
                for e in range(tj)], axis=1)
            rhs_w = jnp.concatenate([dvm[q].reshape(tj * n, n), dvm[q + 1].reshape(tj * n, n)], axis=1)
            prod = jnp.dot(lhs, rhs_w, preferred_element_type=F32)
            wbuf[q] += prod[0:tj, 0:n]
            wbuf[q + 1] += prod[tj:2 * tj, n:2 * n]

    coarse_rhs = hdot(rhs2, RE)
    bc_wait(0, "recv")
    rim_wait(0, "recv")
    rim_wait(2, "recv")

    cext[elems:elems + h] = chalo[...]
    lens = msgs[0, :, 0, :][:, 0:1]
    start_len = jnp.sqrt(jnp.sum(lens, axis=0, keepdims=True))
    inv_len = 1.0 / start_len
    n_one = lens * inv_len * inv_len
    v1 = rhs2 * inv_len
    v1_halo = jnp.where(valid, halos[0] * inv_len, 0.0)
    lines1 = [p * inv_len for p in three_lines(0)]
    coarse1 = coarse_rhs * inv_len
    z1, z1_rim = precondition(v1, v1_halo, lines1, coarse1)
    for c in dcopies:
        c.wait()
    operator(z1, z1_rim)
    fill_sends(1, wbuf)
    start_all(rim_copies(1))
    w1 = wbuf[...].reshape(elems, n)
    own_n1 = total(v1 * v1)
    dot_one = total(v1 * w1)
    p_one = safe_div(dot_one, own_n1)
    gap = w1 - p_one * v1
    msgs[1, me, 0:1] = message([dot_one, p_one, total(gap * gap), own_n1])
    msgs[1, me, 1:2] = packed_rowsum(wbuf[...])
    broadcast(1)
    coarse_w = hdot(w1, RE)
    bc_wait(1, "recv")
    rim_wait(1, "recv")

    X = msgs[1, :, 0, :]
    h11 = jnp.sum(X[:, 0:1], axis=0, keepdims=True)
    dev = X[:, 1:2] - h11
    h21 = jnp.sqrt(jnp.sum(X[:, 2:3] + dev * dev * X[:, 3:4], axis=0, keepdims=True))
    inv21 = 1.0 / h21
    v2 = (w1 - h11 * v1) * inv21
    v2_halo = jnp.where(valid, (halos[1] - h11 * v1_halo) * inv21, 0.0)
    lines2 = [(pw - h11 * pv) * inv21 for pw, pv in zip(three_lines(1), lines1)]
    z2, z2_rim = precondition(v2, v2_halo, lines2, (coarse_w - h11 * coarse1) * inv21)
    operator(z2, z2_rim)
    w2 = wbuf[...].reshape(elems, n)
    alpha = safe_div(total(v1 * v2), own_n1)
    q2 = v2 - alpha * v1
    nq = total(q2 * q2)
    d1 = total(w2 * v1)
    d2 = total(w2 * v2)
    p1 = safe_div(d1, own_n1)
    p2 = safe_div(d2 - alpha * d1, nq)
    gap2 = w2 - p1 * v1 - p2 * q2
    msgs[2, me, 0:1] = message([d1, d2, alpha, nq, p1, p2, total(gap2 * gap2), own_n1])
    msgs[2, me, 1:2] = jnp.zeros((1, n), F32)
    broadcast(2)
    bc_wait(2, "recv")
    Y = msgs[2, :, 0, :]
    h12 = jnp.sum(Y[:, 0:1], axis=0, keepdims=True)
    h22 = jnp.sum(Y[:, 1:2], axis=0, keepdims=True)
    t1 = Y[:, 4:5] - h12 - h22 * Y[:, 2:3]
    t2 = Y[:, 5:6] - h22
    h32 = jnp.sqrt(jnp.sum(t1 * t1 * Y[:, 7:8] + t2 * t2 * Y[:, 3:4] + Y[:, 6:7], axis=0, keepdims=True))

    first = jnp.sqrt(h11 * h11 + h21 * h21)
    cos_one = h11 / first
    sin_one = h21 / first
    upper = cos_one * h12 + sin_one * h22
    lower = -sin_one * h12 + cos_one * h22
    second = jnp.sqrt(lower * lower + h32 * h32)
    cos_two = lower / second
    y2 = cos_two * (-sin_one * start_len) / second
    y1 = (cos_one * start_len - upper * y2) / first
    out[...] = (y1 * z1 + y2 * z2).reshape(ti, tj, n)
    hr, hc = iota((2, 3), 1), iota((2, 3), 0)
    hess_out[...] = jnp.where(
        hr == 0, jnp.where(hc == 0, h11, h12),
        jnp.where(hr == 1, jnp.where(hc == 0, h21, h22), jnp.where(hc == 0, 0.0, h32)))

    for g in range(3):
        bc_wait(g, "send")
        rim_wait(g, "send")


def hand_on(sol_in, hess_in, sol_out, hess_out):
    sol_out[...] = sol_in[...]
    hess_out[...] = hess_in[...]


def solution(mesh):
    nx, ny = mesh.shape["gx"], mesh.shape["gy"]

    def body(rhs, diag, lift, state, basis, cinv):
        ti, tj, n = rhs.shape
        kc = basis.shape[1]
        cflat = jnp.transpose(cinv, (0, 2, 3, 1)).reshape(ti, kc * kc, tj)
        sflat = jnp.transpose(state, (0, 2, 1))
        hrows = 2 * tj + 4 * ti + 32
        h = 2 * ti + 2 * tj
        vm = pl.BlockSpec(memory_space=pltpu.VMEM)
        hbm = pl.BlockSpec(memory_space=pltpu.HBM)
        sol, hess = pl.pallas_call(
            functools.partial(kernel, nx, ny, ti, tj, n, kc),
            out_shape=(jax.ShapeDtypeStruct((ti, tj, n), F32), jax.ShapeDtypeStruct((2, 3), F32)),
            in_specs=[hbm] * 6,
            out_specs=(vm, vm),
            scratch_shapes=[
                pltpu.VMEM((ti, tj, n), F32),
                pltpu.VMEM((4, n, n), BF16),
                pltpu.VMEM((ti, 4, tj), jnp.int32),
                pltpu.VMEM((kc, n), F32),
                pltpu.VMEM((ti, kc * kc, tj), F32),
                pltpu.VMEM((ti, tj, n, n), BF16),
                pltpu.VMEM((8 * n, n), BF16),
                pltpu.VMEM((8, ti * tj, n), F32),
                pltpu.VMEM((ti * tj + h, n), F32),
                pltpu.VMEM((ti, tj, n), F32),
                pltpu.VMEM((2, hrows, n), F32),
                pltpu.VMEM((2, hrows, n), F32),
                pltpu.VMEM((h, n), F32),
                pltpu.VMEM((h, n), F32),
                pltpu.VMEM((3, nx * ny, 2, n), F32),
                pltpu.SemaphoreType.DMA((5,)),
                pltpu.SemaphoreType.DMA((ti,)),
                pltpu.SemaphoreType.DMA((3, 8)),
                pltpu.SemaphoreType.DMA((3, 8)),
                pltpu.SemaphoreType.DMA((3,)),
                pltpu.SemaphoreType.DMA((3,)),
            ],
            compiler_params=pltpu.CompilerParams(collective_id=0, has_side_effects=True,
                                                 vmem_limit_bytes=60 * 1024 * 1024),
        )(rhs, diag, lift, sflat, basis.T, cflat)
        sol, hess = pl.pallas_call(
            hand_on,
            out_shape=(jax.ShapeDtypeStruct(sol.shape, F32), jax.ShapeDtypeStruct(hess.shape, F32)),
            in_specs=[vm, vm],
            out_specs=(vm, vm),
            compiler_params=pltpu.CompilerParams(vmem_limit_bytes=60 * 1024 * 1024),
        )(sol, hess)
        return sol, hess.T

    in_specs = (P("gx", "gy", None), P("gx", "gy", None, None), P(), P("gx", "gy", None), P(),
                P("gx", "gy", None, None))
    return jax.shard_map(body, mesh=mesh, in_specs=in_specs, out_specs=(P("gx", "gy", None), P()), check_vma=False)
```
